32 devices in a mesh: fields: 2 (over y), rows: 4 (over z), cols: 2 (over x), sub: 2 (over core).
Axes of the slice: x: 2, y: 2, z: 4, core: 2. Of those that a mesh axis runs over, the one named last changes fastest.
Arguments:
- convergence: bfloat16 [32, 32, 16, 512], P(('fields', 'rows'), 'cols'), parts along dimension 0, may hold values from -6 to 6
- block_level: int32 [32, 32], P(('fields', 'rows'), 'cols'), parts along dimension 0, may hold values from 0 to 1
- near_codes: int32 [32, 32, 8], P(('fields', 'rows'), 'cols', 'sub'), parts along dimension 0, may hold values from 0 to 24, as said below
- far_rows: int32 [32, 32, 4], P(('fields', 'rows'), 'cols', 'sub'), parts along dimension 0, may hold values from 0 to 15, as said below
- near_factor: bfloat16 [512, 4096], P(None, 'sub'), may hold values from -0.09375 to 0.09375
- far_factor: bfloat16 [512, 2048], P(None, 'sub'), may hold values from -0.125 to 0.125
Outputs:
- whitened: bfloat16 [32, 32, 16, 512], P(('fields', 'rows'), 'cols', 'sub'), parts along dimension 0
The draws below stay inside these ranges and needn't reach their ends.
There are 2 independent parts, one for each index of `fields`. The reference program is written for one: setup_inputs(seed, part) draws one part's arguments, and reference() takes and returns one part's arrays. A program takes and returns all parts, laid end to end along the dimension named above; an argument that names none is the same for every part. Nothing has to cross between parts.
Inputs may be any that keep to these rules, and one draw needn't show every extreme that they name: `near_codes`: the 8 codes of a block are different from one another and never 12 (the block itself). `far_rows`: an entry never names a block row held by the same index of rows as the block. Among the 128 entries that one index of rows, cols and sub holds (slots 0 to 1 or 2 to 3), each other index of rows is named at most 64 times through its block rows, and one is named exactly 64 times.
All inputs are finite; a program needn't handle non-finite values.
Results may differ from the reference program's by a relative error of at most 0.001.
Values may be sent and summed in bfloat16 or wider, within the bound.
A program may use at most 64 MiB of HBM per device.

```python
import jax
import jax.numpy as jnp
from jax import lax

PIX = 512
NEAR = 8
FAR = 4
SAMPLES = 16
TILE_ROWS = 4
TILE_COLS = 16
BROWS = 16
BCOLS = 32
CAP = 64
N_ROWS = 4
N_COLS = 2


def draw_near_codes(key, part):
    scores = jax.random.randint(key, (BROWS, BCOLS, 24), 0, 2 ** 20) * 32 + jnp.arange(24, dtype=jnp.int32)
    ranked = jnp.argsort(scores, axis=-1)[..., :NEAR]
    return (ranked + (ranked >= 12)).astype(jnp.int32)


def draw_far_rows(key, part):
    group_count = N_ROWS * N_COLS * 2
    per_group = 2 * TILE_ROWS * TILE_COLS
    group_keys = jax.random.split(key, group_count)

    def draw_group(group_key, group_index):
        own_row = group_index // (N_COLS * 2)
        key_hot, key_pool, key_mix, key_inner = jax.random.split(group_key, 4)
        hot_source = jax.random.randint(key_hot, (), 0, N_ROWS - 1)
        spare_pool = jnp.arange((N_ROWS - 2) * CAP, dtype=jnp.int32) // CAP
        spare_pool = spare_pool + (spare_pool >= hot_source)
        spare_pool = jax.random.permutation(key_pool, spare_pool)[:per_group - CAP]
        chosen = jnp.concatenate([jnp.zeros((CAP,), jnp.int32) + hot_source, spare_pool])
        chosen = jax.random.permutation(key_mix, chosen)
        device = chosen + (chosen >= own_row)
        row_within = jax.random.randint(key_inner, (per_group,), 0, TILE_ROWS)
        return (device * TILE_ROWS + row_within).astype(jnp.int32)
    drawn = jax.vmap(draw_group)(group_keys, jnp.arange(group_count, dtype=jnp.int32))
    drawn = drawn.reshape(N_ROWS, N_COLS, 2, TILE_ROWS, TILE_COLS, 2)
    drawn = jnp.transpose(drawn, (0, 3, 1, 4, 2, 5))
    return drawn.reshape(BROWS, BCOLS, FAR).astype(jnp.int32)


def plant(array, stream_key, smallest, high):
    longest = array.shape.index(max(array.shape))
    spots = []
    for shift in (0, 1):
        where = [jax.random.randint(jax.random.fold_in(stream_key, axis), (), 0, length) for axis, length in enumerate(array.shape)]
        where[longest] = (where[longest] + shift) % array.shape[longest]
        spots.append(tuple(where))
    return array.at[spots[0]].set(smallest).at[spots[1]].set(high)


def shard_levels(own_key, shape, cuts, smallest, high):
    level = 1.0
    for dim, shards_of in cuts:
        steps = jax.random.uniform(jax.random.fold_in(jax.random.fold_in(own_key, 6), dim), (shards_of,), jnp.float32, smallest / len(cuts), high / len(cuts))
        level = level * jnp.repeat(jnp.exp(steps), shape[dim] // shards_of).reshape((-1,) + (1,) * (len(shape) - 1 - dim))
    return level


def scatter_about(rng, shape, scale, reach, cuts=(), held_as=jnp.bfloat16):
    array = jax.random.normal(rng, shape, jnp.float32) * scale
    if len(cuts) > 0:
        array = shard_levels(rng, shape, cuts, -0.22, 0.18) * array
    return jnp.clip(array, min=-reach, max=reach).astype(held_as)


def setup_inputs(seed: int = 0, part: int = 0) -> dict:
    key_of = jax.random.split(jax.random.key(seed), 7)
    part_keys = jax.random.split(jax.random.fold_in(key_of[6], part), 7)
    convergence = scatter_about(part_keys[0], (BROWS, BCOLS, SAMPLES, PIX), 1.0, 6.0, ((0, 4), (1, 2)))
    block_level = plant(jax.random.randint(part_keys[1], (BROWS, BCOLS), 0, 2), jax.random.fold_in(part_keys[1], 1), 0, 1).astype(jnp.int32)
    near_codes = draw_near_codes(jax.random.fold_in(jax.random.fold_in(key_of[6], part), 71), part)
    far_rows = draw_far_rows(jax.random.fold_in(jax.random.fold_in(key_of[6], part), 71), part)
    near_factor = scatter_about(key_of[4], (PIX, NEAR * PIX), (NEAR * PIX) ** -0.5, 0.09375, ((1, 2),))
    far_factor = scatter_about(key_of[5], (PIX, FAR * PIX), (FAR * PIX) ** -0.5, 0.125, ((1, 2),))
    return {"convergence": convergence, "block_level": block_level, "near_codes": near_codes, "far_rows": far_rows, "near_factor": near_factor, "far_factor": far_factor}


def reference(convergence, block_level, near_codes, far_rows, near_factor, far_factor):
    padded = jnp.pad(convergence, ((2, 2), (2, 2), (0, 0), (0, 0)))
    near_weight = near_factor.astype(jnp.float32).reshape(PIX, NEAR, PIX)
    far_weight = far_factor.astype(jnp.float32).reshape(PIX, FAR, PIX)
    columns = jnp.arange(BCOLS, dtype=jnp.int32)

    def one_row(row):
        codes = near_codes[row]
        row_index = (row + codes // 5).astype(jnp.int32)
        col_index = (columns[:, None] + codes % 5).astype(jnp.int32)
        near_blocks = padded[row_index, col_index].astype(jnp.float32)
        near_term = jnp.einsum("cksq,pkq->csp", near_blocks, near_weight)
        far_blocks = convergence[far_rows[row].astype(jnp.int32), columns[:, None]].astype(jnp.float32)
        far_term = jnp.einsum("cksq,pkq->csp", far_blocks, far_weight)
        mean = jnp.where(block_level[row][:, None, None] == 1, near_term, far_term)
        return (convergence[row].astype(jnp.float32) - mean).astype(jnp.bfloat16)

    return lax.map(one_row, jnp.arange(BROWS, dtype=jnp.int32))
```

```python
import functools

import jax
import jax.numpy as jnp
from jax import lax
from jax.experimental import pallas as pl
from jax.experimental.pallas import tpu as pltpu
from jax.sharding import PartitionSpec as P

MESH = pl.DeviceIdType.MESH
CHUNKS = 4
ROW_STRIDE_BITS = 8


def kernel(dims, conv, codes, near_factor, far_factor, out, *scratch):
    n_rows, n_cols, tile_rows, tile_cols, half, pixels, near_slots, far_slots, chunks = dims
    chunk_cols = tile_cols // chunks
    far = scratch[:chunks]
    (near, near_w, far_w, codes_v, codes_s, near_g, far_g, near_acc, far_acc,
     white_src, white_dst, tile_send, tile_recv, white_send, white_recv,
     side_send, side_recv, code_send, code_recv, fac_send, fac_recv, loc_sem, halo_sem) = scratch[chunks:]

    i = lax.axis_index("rows")
    x = lax.axis_index("cols")
    s = lax.axis_index("sub")
    other = 1 - s
    mine = pl.ds(pl.multiple_of(s * half, half), half)
    is_end = (i == 0) | (i == n_rows - 1)
    is_mid = (i > 0) & (i < n_rows - 1)
    low_helper = i == 1
    high_helper = i == n_rows - 2
    is_helper = low_helper | high_helper
    end_tile = jnp.where(low_helper, 0, n_rows - 1)
    to_mid = jnp.where(i == 0, 1, n_rows - 2)

    def cols_of(k):
        return pl.ds(k * chunk_cols, chunk_cols)

    local = [
        pltpu.make_async_copy(
            conv.at[:, :, mine, :],
            near.at[pl.ds(2, tile_rows), pl.ds(2, tile_cols)],
            loc_sem.at[0],
        ),
        pltpu.make_async_copy(near_factor, near_w.at[s], loc_sem.at[1]),
        pltpu.make_async_copy(far_factor, far_w.at[s], loc_sem.at[2]),
        pltpu.make_async_copy(codes, codes_s.at[0, s], loc_sem.at[3]),
    ]
    for copy in local:
        copy.start()
    own_far = [
        pltpu.make_async_copy(
            conv.at[:, cols_of(k), mine, :],
            far[k].at[pl.ds(i * tile_rows, tile_rows)],
            loc_sem.at[6 + k],
        )
        for k in range(chunks)
    ]

    @pl.when(is_mid)
    def _():
        for copy in own_far:
            copy.start()

    @pl.when(i == 0)
    def _():
        near[0:2] = jnp.zeros((2,) + near.shape[1:], near.dtype)

    @pl.when(i == n_rows - 1)
    def _():
        near[tile_rows + 2:tile_rows + 4] = jnp.zeros((2,) + near.shape[1:], near.dtype)

    @pl.when(x == 0)
    def _():
        near[:, 0:2] = jnp.zeros((near.shape[0], 2) + near.shape[2:], near.dtype)

    @pl.when(x == n_cols - 1)
    def _():
        near[:, tile_cols + 2:tile_cols + 4] = jnp.zeros((near.shape[0], 2) + near.shape[2:], near.dtype)

    barrier = pltpu.get_barrier_semaphore()
    offsets = [(di, dx) for di in (-1, 0, 1) for dx in (-1, 0, 1) if (di, dx) != (0, 0)]

    def present(di, dx):
        ok = jnp.bool_(True)
        if di == -1:
            ok = ok & (i > 0)
        if di == 1:
            ok = ok & (i < n_rows - 1)
        if dx == -1:
            ok = ok & (x > 0)
        if dx == 1:
            ok = ok & (x < n_cols - 1)
        return ok

    for di, dx in offsets:
        @pl.when(present(di, dx))
        def _():
            pl.semaphore_signal(barrier, inc=1, device_id={"rows": i + di, "cols": x + dx}, device_id_type=MESH)
    for di in (-1, 0, 1):
        @pl.when(present(di, 0))
        def _():
            pl.semaphore_signal(barrier, inc=1, device_id={"rows": i + di, "sub": other}, device_id_type=MESH)
    count_z = (i > 0).astype(jnp.int32) + (i < n_rows - 1).astype(jnp.int32) + 1
    count_x = (x > 0).astype(jnp.int32) + (x < n_cols - 1).astype(jnp.int32) + 1
    pl.semaphore_wait(barrier, count_z * count_x - 1 + count_z)

    def code_copy(which, slot, target):
        return pltpu.make_async_remote_copy(
            src_ref=codes, dst_ref=codes_v.at[slot, s], send_sem=code_send.at[which],
            recv_sem=code_recv.at[which], device_id=target, device_id_type=MESH)

    code_partner = code_copy(0, 0, {"sub": other})
    code_straight = code_copy(1, 1, {"rows": to_mid})
    code_cross = code_copy(2, 1, {"rows": to_mid, "sub": other})
    code_partner.start()

    @pl.when(is_end)
    def _():
        code_straight.start()
        code_cross.start()

    def side_copy(di, dx):
        if di == 0:
            rows_src, rows_dst = pl.ds(0, tile_rows), pl.ds(2, tile_rows)
        elif di == -1:
            rows_src, rows_dst = pl.ds(0, 2), pl.ds(tile_rows + 2, 2)
        else:
            rows_src, rows_dst = pl.ds(tile_rows - 2, 2), pl.ds(0, 2)
        if dx == 0:
            cols_src, cols_dst = pl.ds(0, tile_cols), pl.ds(2, tile_cols)
        elif dx == -1:
            cols_src, cols_dst = pl.ds(0, 2), pl.ds(tile_cols + 2, 2)
        else:
            cols_src, cols_dst = pl.ds(tile_cols - 2, 2), pl.ds(0, 2)
        which = offsets.index((di, dx))
        return pltpu.make_async_remote_copy(
            src_ref=conv.at[rows_src, cols_src, mine, :],
            dst_ref=near.at[rows_dst, cols_dst],
            send_sem=side_send.at[which], recv_sem=side_recv.at[which],
            device_id={"rows": i + di, "cols": x + dx}, device_id_type=MESH)

    def side_sends(di, dx):
        if dx == 0:
            return low_helper if di == -1 else high_helper
        return present(di, dx)

    def side_receives(di, dx):
        if dx == 0:
            return (i == 0) if di == -1 else (i == n_rows - 1)
        return present(-di, -dx)

    def tile_copy(way, d, k, tile):
        src = conv.at[:, cols_of(k), mine, :] if d == 0 else far[k].at[pl.ds(tile * tile_rows, tile_rows)]
        return pltpu.make_async_remote_copy(
            src_ref=src, dst_ref=far[k].at[pl.ds(tile * tile_rows, tile_rows)],
            send_sem=tile_send.at[way, d, k], recv_sem=tile_recv.at[way, d, k],
            device_id={"rows": i - 1 if way == 0 else i + 1}, device_id_type=MESH)

    def sent(way, d, k):
        return tile_copy(way, d, k, i + d if way == 0 else i - d)

    def received(way, d, k):
        return tile_copy(way, d, k, i + 1 + d if way == 0 else i - 1 - d)

    def tile_sends(way, d):
        if way == 0:
            return (i >= 2) & (i + d <= n_rows - 1)
        return (i <= n_rows - 3) & (i - d >= 0)

    def tile_receives(way, d):
        if way == 0:
            return is_mid & (i + 1 + d <= n_rows - 1)
        return is_mid & (i - 1 - d >= 0)

    for k in range(chunks):
        for way in (0, 1):
            @pl.when(tile_sends(way, 0))
            def _():
                sent(way, 0, k).start()
        if k == 0:
            for di, dx in offsets:
                @pl.when(side_sends(di, dx))
                def _():
                    side_copy(di, dx).start()

    def factor_copy(which):
        src, dst = ((near_factor, near_w), (far_factor, far_w))[which]
        return pltpu.make_async_remote_copy(
            src_ref=src, dst_ref=dst.at[s], send_sem=fac_send.at[which],
            recv_sem=fac_recv.at[which], device_id={"sub": other}, device_id_type=MESH)

    for which in (0, 1):
        factor_copy(which).start()

    def halo_copy(way, k):
        if way == 0:
            src_rows, dst_rows = pl.ds((i + 1) * tile_rows, 2), pl.ds(tile_rows + 2, 2)
        else:
            src_rows, dst_rows = pl.ds(i * tile_rows - 2, 2), pl.ds(0, 2)
        return pltpu.make_async_copy(
            far[k].at[src_rows], near.at[dst_rows, pl.ds(2 + k * chunk_cols, chunk_cols)], halo_sem.at[way, k])

    for d in range(n_rows - 3):
        for k in range(chunks):
            for way in (0, 1):
                @pl.when(tile_receives(way, d))
                def _():
                    received(way, d, k).wait_recv()
                    if d == 0:
                        halo_copy(way, k).start()

                @pl.when(tile_sends(way, d + 1))
                def _():
                    sent(way, d + 1, k).start()

    code_copy(0, 0, {"sub": other}).wait_recv()
    code_in = pltpu.make_async_copy(codes_v.at[0, other], codes_s.at[0, other], loc_sem.at[4])
    code_in.start()
    end_codes = pltpu.make_async_copy(codes_v.at[1], codes_s.at[1], loc_sem.at[5])

    @pl.when(is_helper)
    def _():
        code_straight.wait_recv()
        code_cross.wait_recv()
        end_codes.start()
        end_codes.wait()

    code_in.wait()
    for copy in local:
        copy.wait()
    for which in (0, 1):
        factor_copy(which).wait_recv()

    @pl.when(is_mid)
    def _():
        for k in range(chunks):
            halo_copy(0, k).wait()
            halo_copy(1, k).wait()
            own_far[k].wait()

    for di, dx in offsets:
        @pl.when(side_receives(di, dx))
        def _():
            side_copy(di, dx).wait_recv()

    pairs = tile_cols // 2

    def gather_near(t, carry):
        r = t // pairs
        c = (t % pairs) * 2
        at = pl.ds(pl.multiple_of(t * 2 * half, 2 * half), 2 * half)
        for sub in range(2):
            for slot in range(near_slots):
                parts = []
                for step in range(2):
                    place = codes_s[0, sub, r, (c + step) * near_slots + slot]
                    row = lax.shift_right_logical(place, ROW_STRIDE_BITS)
                    col = place & ((1 << ROW_STRIDE_BITS) - 1)
                    parts.append(near[row, col].astype(jnp.float32))
                near_g[sub * near_slots + slot, at, :] = jnp.concatenate(parts, axis=0).astype(jnp.bfloat16)
        return carry

    lax.fori_loop(0, tile_rows * pairs, gather_near, 0)
    contract = (((1,), (1,)), ((), ()))

    def near_dot(first, sub, slot):
        where = pl.ds(pl.multiple_of(slot * pixels, pixels), pixels)
        product = lax.dot_general(
            near_g[sub * near_slots + slot], near_w[sub, :, where], contract, preferred_element_type=jnp.float32)
        if first:
            near_acc[...] = product
        else:
            near_acc[...] += product

    near_dot(True, 0, 0)

    def near_step(t, carry):
        near_dot(False, t // near_slots, t % near_slots)
        return carry

    lax.fori_loop(1, 2 * near_slots, near_step, 0)

    level_at = tile_cols * (near_slots + far_slots)
    far_at = tile_cols * near_slots
    chunk_blocks = tile_rows * chunk_cols
    chunk_rows = chunk_blocks * half

    def block_rows(block):
        return pl.ds(pl.multiple_of(block * half, half), half)

    def far_chunk(k):
        def gather_far(who, base):
            def body(t, carry):
                at = pl.ds(pl.multiple_of(base + t * 2 * half, 2 * half), 2 * half)
                for sub in range(2):
                    for slot in range(far_slots):
                        parts = []
                        for step in range(2):
                            block = 2 * t + step
                            r, c = block // chunk_cols, block % chunk_cols
                            row = codes_s[who, sub, r, far_at + (k * chunk_cols + c) * far_slots + slot]
                            parts.append(far[k][row, c].astype(jnp.float32))
                        far_g[sub * far_slots + slot, at, :] = jnp.concatenate(parts, axis=0).astype(jnp.bfloat16)
                return carry

            lax.fori_loop(0, chunk_blocks // 2, body, 0)

        gather_far(0, 0)

        @pl.when(is_helper)
        def _():
            gather_far(1, chunk_rows)

        for sub in range(2):
            for slot in range(far_slots):
                product = lax.dot_general(
                    far_g[sub * far_slots + slot], far_w[sub, :, slot * pixels:(slot + 1) * pixels],
                    contract, preferred_element_type=jnp.float32)
                if sub + slot == 0:
                    far_acc[...] = product
                else:
                    far_acc[...] += product

        @pl.when(is_helper)
        def _():
            def body(block, carry):
                r, c = block // chunk_cols, block % chunk_cols
                value = far[k][end_tile * tile_rows + r, c].astype(jnp.float32)
                mean = far_acc[block_rows(chunk_blocks + block), :]
                white_src[r, k * chunk_cols + c] = (value - mean).astype(jnp.bfloat16)
                return carry

            lax.fori_loop(0, chunk_blocks, body, 0)
            white_copy(k).start()

        def body(block, carry):
            r, c = block // chunk_cols, block % chunk_cols
            col = k * chunk_cols + c
            level = codes_s[0, 0, r, level_at + col]
            mean = jnp.where(level == 1, near_acc[block_rows(r * tile_cols + col), :], far_acc[block_rows(block), :])
            out[r, col] = (near[2 + r, 2 + col].astype(jnp.float32) - mean).astype(jnp.bfloat16)
            return carry

        lax.fori_loop(0, chunk_blocks, body, 0)

    def white_copy(k):
        return pltpu.make_async_remote_copy(
            src_ref=white_src.at[:, cols_of(k)], dst_ref=white_dst.at[:, cols_of(k)],
            send_sem=white_send.at[k], recv_sem=white_recv.at[k],
            device_id={"rows": end_tile}, device_id_type=MESH)

    @pl.when(is_mid)
    def _():
        for k in range(chunks):
            d = n_rows - 3
            for way in (0, 1):
                @pl.when(tile_receives(way, d))
                def _():
                    received(way, d, k).wait_recv()
            far_chunk(k)

    @pl.when(is_end)
    def _():
        for k in range(chunks):
            white_copy(k).wait_recv()

            def body(block, carry):
                r, c = block // chunk_cols, block % chunk_cols
                col = k * chunk_cols + c
                level = codes_s[0, 0, r, level_at + col]
                fine = near[2 + r, 2 + col].astype(jnp.float32) - near_acc[block_rows(r * tile_cols + col), :]
                coarse = white_dst[r, col].astype(jnp.float32)
                out[r, col] = jnp.where(level == 1, fine, coarse).astype(jnp.bfloat16)
                return carry

            lax.fori_loop(0, chunk_blocks, body, 0)

    code_partner.wait_send()

    @pl.when(is_end)
    def _():
        code_straight.wait_send()
        code_cross.wait_send()

    for di, dx in offsets:
        @pl.when(side_sends(di, dx))
        def _():
            side_copy(di, dx).wait_send()
    for which in (0, 1):
        factor_copy(which).wait_send()
    for d in range(n_rows - 2):
        for way in (0, 1):
            @pl.when(tile_sends(way, d))
            def _():
                for k in range(chunks):
                    sent(way, d, k).wait_send()

    @pl.when(is_helper)
    def _():
        for k in range(chunks):
            white_copy(k).wait_send()


def on_device(convergence, block_level, near_codes, far_rows, near_factor, far_factor):
    tile_rows, tile_cols, samples, pixels = convergence.shape
    n_rows, n_cols = lax.axis_size("rows"), lax.axis_size("cols")
    near_slots, far_slots = near_codes.shape[2], far_rows.shape[2]
    half = samples // 2
    chunks = CHUNKS
    chunk_cols = tile_cols // chunks
    row_pos = jnp.arange(tile_rows, dtype=jnp.int32)[:, None, None]
    col_pos = jnp.arange(tile_cols, dtype=jnp.int32)[None, :, None]
    places = (row_pos + near_codes // 5) * (1 << ROW_STRIDE_BITS) + col_pos + near_codes % 5
    codes = jnp.concatenate(
        [places.reshape(tile_rows, -1), far_rows.reshape(tile_rows, -1), block_level], axis=1)
    width = codes.shape[1]
    codes = jnp.pad(codes, ((0, 0), (0, -width % 128)))
    dims = (n_rows, n_cols, tile_rows, tile_cols, half, pixels, near_slots, far_slots, chunks)
    block = (half, pixels)
    bf16, f32 = jnp.bfloat16, jnp.float32
    chunk_rows = tile_rows * chunk_cols * half
    dma = pltpu.SemaphoreType.DMA
    scratch = [pltpu.VMEM((n_rows * tile_rows, chunk_cols) + block, bf16) for _ in range(chunks)]
    scratch += [
        pltpu.VMEM((tile_rows + 4, tile_cols + 4) + block, bf16),
        pltpu.VMEM((2,) + near_factor.shape, bf16),
        pltpu.VMEM((2,) + far_factor.shape, bf16),
        pltpu.VMEM((2, 2) + codes.shape, jnp.int32),
        pltpu.SMEM((2, 2) + codes.shape, jnp.int32),
        pltpu.VMEM((2 * near_slots, tile_rows * tile_cols * half, pixels), bf16),
        pltpu.VMEM((2 * far_slots, 2 * chunk_rows, pixels), bf16),
        pltpu.VMEM((tile_rows * tile_cols * half, pixels), f32),
        pltpu.VMEM((2 * chunk_rows, pixels), f32),
        pltpu.VMEM((tile_rows, tile_cols) + block, bf16),
        pltpu.VMEM((tile_rows, tile_cols) + block, bf16),
        dma((2, n_rows - 2, chunks)),
        dma((2, n_rows - 2, chunks)),
        dma((chunks,)),
        dma((chunks,)),
        dma((8,)),
        dma((8,)),
        dma((3,)),
        dma((3,)),
        dma((2,)),
        dma((2,)),
        dma((6 + chunks,)),
        dma((2, chunks)),
    ]
    anywhere = pl.BlockSpec(memory_space=pl.ANY)
    vmem = pl.BlockSpec(memory_space=pltpu.VMEM)
    return pl.pallas_call(
        functools.partial(kernel, dims),
        out_shape=jax.ShapeDtypeStruct((tile_rows, tile_cols) + block, bf16),
        in_specs=[anywhere, vmem, anywhere, anywhere],
        out_specs=vmem,
        scratch_shapes=scratch,
        compiler_params=pltpu.CompilerParams(
            collective_id=0, has_side_effects=True, vmem_limit_bytes=56 * 1024 * 1024),
    )(convergence, codes, near_factor, far_factor)


def solution(mesh):
    placed = (
        P(("fields", "rows"), "cols", None, None),
        P(("fields", "rows"), "cols"),
        P(("fields", "rows"), "cols", "sub"),
        P(("fields", "rows"), "cols", "sub"),
        P(None, "sub"),
        P(None, "sub"),
    )
    return jax.shard_map(
        on_device,
        mesh=mesh,
        in_specs=placed,
        out_specs=P(("fields", "rows"), "cols", "sub", None),
        check_vma=False,
    )
```

```python
import functools

import jax
import jax.numpy as jnp
from jax import lax
from jax.experimental import pallas as pl
from jax.experimental.pallas import tpu as pltpu
from jax.sharding import PartitionSpec as P

MESH = pl.DeviceIdType.MESH
PARTS = 4


def chunk_starts(cols):
    return [0, cols * 5 // 16, cols * 10 // 16, cols * 14 // 16, cols]


def kernel(dims, conv, codes, near_factor, far_factor, out, *scratch):
    n_rows, n_cols, tile_rows, tile_cols, half, pixels, near_slots, far_slots = dims
    starts = chunk_starts(tile_cols)
    chunks = len(starts) - 1
    sizes = [starts[k + 1] - starts[k] for k in range(chunks)]
    far = scratch[:chunks]
    (near, near_w, far_w, codes_v, codes_s, near_g, far_g, near_acc, far_acc, end_acc,
     white_src, white_dst, tile_send, tile_recv, white_send, white_recv,
     side_send, side_recv, corner_send, corner_recv, code_send, code_recv, fac_send, fac_recv, loc_sem, halo_sem) = scratch[chunks:]

    i = lax.axis_index("rows")
    x = lax.axis_index("cols")
    s = lax.axis_index("sub")
    other = 1 - s
    mine = pl.ds(pl.multiple_of(s * half, half), half)
    is_end = (i == 0) | (i == n_rows - 1)
    is_mid = (i > 0) & (i < n_rows - 1)
    low_helper = i == 1
    high_helper = i == n_rows - 2
    is_helper = low_helper | high_helper
    end_tile = jnp.where(low_helper, 0, n_rows - 1)
    to_mid = jnp.where(i == 0, 1, n_rows - 2)

    def cols_of(k):
        return pl.ds(starts[k], sizes[k])

    local = [
        pltpu.make_async_copy(
            conv.at[:, :, mine, :],
            near.at[pl.ds(2, tile_rows), pl.ds(2, tile_cols)],
            loc_sem.at[0],
        ),
        pltpu.make_async_copy(near_factor, near_w.at[s], loc_sem.at[1]),
        pltpu.make_async_copy(far_factor, far_w.at[s], loc_sem.at[2]),
        pltpu.make_async_copy(codes, codes_s.at[0, s], loc_sem.at[3]),
    ]
    for copy in local:
        copy.start()
    own_far = [
        pltpu.make_async_copy(
            conv.at[:, cols_of(k), mine, :],
            far[k].at[pl.ds(i * tile_rows, tile_rows)],
            loc_sem.at[6 + k],
        )
        for k in range(chunks)
    ]

    @pl.when(is_mid)
    def _():
        for copy in own_far:
            copy.start()

    @pl.when(i == 0)
    def _():
        near[0:2] = jnp.zeros((2,) + near.shape[1:], near.dtype)

    @pl.when(i == n_rows - 1)
    def _():
        near[tile_rows + 2:tile_rows + 4] = jnp.zeros((2,) + near.shape[1:], near.dtype)

    @pl.when(x == 0)
    def _():
        near[:, 0:2] = jnp.zeros((near.shape[0], 2) + near.shape[2:], near.dtype)

    @pl.when(x == n_cols - 1)
    def _():
        near[:, tile_cols + 2:tile_cols + 4] = jnp.zeros((near.shape[0], 2) + near.shape[2:], near.dtype)

    barrier = pltpu.get_barrier_semaphore()
    offsets = [(-1, 0), (1, 0), (0, -1), (0, 1)]

    def present(di, dx):
        ok = jnp.bool_(True)
        if di == -1:
            ok = ok & (i > 0)
        if di == 1:
            ok = ok & (i < n_rows - 1)
        if dx == -1:
            ok = ok & (x > 0)
        if dx == 1:
            ok = ok & (x < n_cols - 1)
        return ok

    for di, dx in offsets:
        @pl.when(present(di, dx))
        def _():
            pl.semaphore_signal(barrier, inc=1, device_id={"rows": i + di, "cols": x + dx}, device_id_type=MESH)
    pl.semaphore_signal(barrier, inc=1, device_id={"sub": other}, device_id_type=MESH)
    count_z = (i > 0).astype(jnp.int32) + (i < n_rows - 1).astype(jnp.int32)
    count_x = (x > 0).astype(jnp.int32) + (x < n_cols - 1).astype(jnp.int32)
    pl.semaphore_wait(barrier, count_z + count_x + 1)

    def code_copy(which, slot, target):
        return pltpu.make_async_remote_copy(
            src_ref=codes if which < 2 else codes_v.at[slot, s], dst_ref=codes_v.at[slot, s],
            send_sem=code_send.at[which], recv_sem=code_recv.at[which], device_id=target, device_id_type=MESH)

    code_partner = code_copy(0, 0, {"sub": other})
    code_straight = code_copy(1, 1, {"rows": to_mid})
    code_relay = code_copy(2, 1, {"sub": other})
    code_partner.start()

    @pl.when(is_end)
    def _():
        code_straight.start()

    def side_copy(di, dx):
        if di == 0:
            rows_src, rows_dst = pl.ds(0, tile_rows), pl.ds(2, tile_rows)
        elif di == -1:
            rows_src, rows_dst = pl.ds(0, 2), pl.ds(tile_rows + 2, 2)
        else:
            rows_src, rows_dst = pl.ds(tile_rows - 2, 2), pl.ds(0, 2)
        if dx == 0:
            cols_src, cols_dst = pl.ds(0, tile_cols), pl.ds(2, tile_cols)
        elif dx == -1:
            cols_src, cols_dst = pl.ds(0, 2), pl.ds(tile_cols + 2, 2)
        else:
            cols_src, cols_dst = pl.ds(tile_cols - 2, 2), pl.ds(0, 2)
        which = offsets.index((di, dx))
        return pltpu.make_async_remote_copy(
            src_ref=conv.at[rows_src, cols_src, mine, :],
            dst_ref=near.at[rows_dst, cols_dst],
            send_sem=side_send.at[which], recv_sem=side_recv.at[which],
            device_id={"rows": i + di, "cols": x + dx}, device_id_type=MESH)

    def side_sends(di, dx):
        if dx == 0:
            return low_helper if di == -1 else high_helper
        return present(di, dx)

    def side_receives(di, dx):
        if dx == 0:
            return (i == 0) if di == -1 else (i == n_rows - 1)
        return present(-di, -dx)

    def tile_copy(way, d, k, tile):
        src = conv.at[:, cols_of(k), mine, :] if d == 0 else far[k].at[pl.ds(tile * tile_rows, tile_rows)]
        return pltpu.make_async_remote_copy(
            src_ref=src, dst_ref=far[k].at[pl.ds(tile * tile_rows, tile_rows)],
            send_sem=tile_send.at[way, d, k], recv_sem=tile_recv.at[way, d, k],
            device_id={"rows": i - 1 if way == 0 else i + 1}, device_id_type=MESH)

    def sent(way, d, k):
        return tile_copy(way, d, k, i + d if way == 0 else i - d)

    def received(way, d, k):
        return tile_copy(way, d, k, i + 1 + d if way == 0 else i - 1 - d)

    def tile_sends(way, d):
        if way == 0:
            return (i >= 2) & (i + d <= n_rows - 1)
        return (i <= n_rows - 3) & (i - d >= 0)

    def tile_receives(way, d):
        if way == 0:
            return is_mid & (i + 1 + d <= n_rows - 1)
        return is_mid & (i - 1 - d >= 0)

    for k in range(chunks):
        for way in (0, 1):
            @pl.when(tile_sends(way, 0))
            def _():
                sent(way, 0, k).start()
        if k == 0:
            for di, dx in offsets:
                @pl.when(side_sends(di, dx))
                def _():
                    side_copy(di, dx).start()

    def factor_copy(which):
        src, dst = ((near_factor, near_w), (far_factor, far_w))[which]
        return pltpu.make_async_remote_copy(
            src_ref=src, dst_ref=dst.at[s], send_sem=fac_send.at[which],
            recv_sem=fac_recv.at[which], device_id={"sub": other}, device_id_type=MESH)

    for which in (0, 1):
        factor_copy(which).start()

    def halo_copy(way, k):
        if way == 0:
            src_rows, dst_rows = pl.ds((i + 1) * tile_rows, 2), pl.ds(tile_rows + 2, 2)
        else:
            src_rows, dst_rows = pl.ds(i * tile_rows - 2, 2), pl.ds(0, 2)
        return pltpu.make_async_copy(
            far[k].at[src_rows], near.at[dst_rows, pl.ds(2 + starts[k], sizes[k])], halo_sem.at[way, k])

    for d in range(n_rows - 3):
        for k in range(chunks):
            for way in (0, 1):
                @pl.when(tile_receives(way, d))
                def _():
                    received(way, d, k).wait_recv()
                    if d == 0:
                        halo_copy(way, k).start()

                @pl.when(tile_sends(way, d + 1))
                def _():
                    sent(way, d + 1, k).start()

    code_copy(0, 0, {"sub": other}).wait_recv()
    code_in = pltpu.make_async_copy(codes_v.at[0, other], codes_s.at[0, other], loc_sem.at[4])
    code_in.start()
    end_codes = pltpu.make_async_copy(codes_v.at[1], codes_s.at[1], loc_sem.at[5])

    @pl.when(is_helper)
    def _():
        code_straight.wait_recv()
        code_relay.start()

    for copy in local:
        copy.wait()

    @pl.when(is_mid)
    def _():
        for k in range(chunks):
            halo_copy(0, k).wait()
            halo_copy(1, k).wait()
            own_far[k].wait()

    for di, dx in offsets:
        @pl.when(side_receives(di, dx))
        def _():
            side_copy(di, dx).wait_recv()

    def corner_copy(di, dx):
        rows = pl.ds(0, 2) if di == -1 else pl.ds(tile_rows + 2, 2)
        src, dst = (2, tile_cols + 2) if dx == -1 else (tile_cols, 0)
        which = (di + 1) + (dx + 1) // 2
        return pltpu.make_async_remote_copy(
            src_ref=near.at[rows, pl.ds(src, 2)], dst_ref=near.at[rows, pl.ds(dst, 2)],
            send_sem=corner_send.at[which], recv_sem=corner_recv.at[which],
            device_id={"cols": x + dx}, device_id_type=MESH)

    corners = [(di, dx) for di in (-1, 1) for dx in (-1, 1)]
    for di, dx in corners:
        @pl.when(present(di, 0) & present(0, dx))
        def _():
            corner_copy(di, dx).start()

    @pl.when(is_helper)
    def _():
        code_relay.wait_recv()
        end_codes.start()
        end_codes.wait()

    code_in.wait()
    for which in (0, 1):
        factor_copy(which).wait_recv()
    for di, dx in corners:
        @pl.when(present(di, 0) & present(0, -dx))
        def _():
            corner_copy(di, dx).wait_recv()

    contract = (((1,), (1,)), ((), ()))
    part_slots = 2 * near_slots // PARTS

    def block_rows(block):
        return pl.ds(pl.multiple_of(block * half, half), half)

    def pair_rows(block):
        return pl.ds(pl.multiple_of(block * half, 2 * half), 2 * half)

    def joined(first, second):
        both = jnp.concatenate([first.astype(jnp.float32), second.astype(jnp.float32)], axis=0)
        return both.astype(jnp.bfloat16)

    def near_part(part):
        sub, base = part * part_slots // near_slots, part * part_slots % near_slots

        def near_block(r, c, slot):
            code = codes_s[0, sub, r, base + slot, c]
            down = lax.shift_right_logical(code * 205, 10)
            return near[r + down, c + code - 5 * down]

        def gather(c, carry):
            for r in range(0, tile_rows, 2):
                for slot in range(part_slots):
                    near_g[pair_rows(c * tile_rows + r), slot * pixels:(slot + 1) * pixels] = joined(
                        near_block(r, c, slot), near_block(r + 1, c, slot))
            return carry

        lax.fori_loop(0, tile_cols, gather, 0)
        product = lax.dot_general(
            near_g[...], near_w[sub, :, base * pixels:(base + part_slots) * pixels], contract,
            preferred_element_type=jnp.float32)
        if part == 0:
            near_acc[...] = product
        else:
            near_acc[...] += product

    level_at = near_slots + far_slots

    def far_chunk(k):
        rows = sizes[k] * tile_rows * half

        def gather_far(who):
            def far_block(r, c, sub, slot):
                row = codes_s[who, sub, r, near_slots + slot, starts[k] + c]
                return far[k][row, c]

            def body(c, carry):
                for r in range(0, tile_rows, 2):
                    for sub in range(2):
                        for slot in range(far_slots):
                            at = sub * far_slots + slot
                            far_g[pair_rows((who * sizes[k] + c) * tile_rows + r), at * pixels:(at + 1) * pixels] = joined(
                                far_block(r, c, sub, slot), far_block(r + 1, c, sub, slot))
                return carry

            lax.fori_loop(0, sizes[k], body, 0)

        gather_far(0)

        @pl.when(is_helper)
        def _():
            gather_far(1)

        depth = far_slots * pixels
        product = lax.dot_general(
            far_g[:2 * rows, :depth], far_w[0], contract, preferred_element_type=jnp.float32)
        product += lax.dot_general(
            far_g[:2 * rows, depth:], far_w[1], contract, preferred_element_type=jnp.float32)
        far_acc[pl.ds(starts[k] * tile_rows * half, rows), :] = product[:rows]
        end_acc[pl.ds(0, rows), :] = product[rows:]

        @pl.when(is_helper)
        def _():
            def body(c, carry):
                for r in range(tile_rows):
                    value = far[k][end_tile * tile_rows + r, c].astype(jnp.float32)
                    white_src[r, starts[k] + c] = (value - end_acc[block_rows(c * tile_rows + r), :]).astype(jnp.bfloat16)
                return carry

            lax.fori_loop(0, sizes[k], body, 0)
            white_copy(k).start()

    def white_copy(k):
        return pltpu.make_async_remote_copy(
            src_ref=white_src.at[:, cols_of(k)], dst_ref=white_dst.at[:, cols_of(k)],
            send_sem=white_send.at[k], recv_sem=white_recv.at[k],
            device_id={"rows": end_tile}, device_id_type=MESH)

    @pl.when(is_mid)
    def _():
        near_part(0)
        for k in range(chunks):
            d = n_rows - 3
            for way in (0, 1):
                @pl.when(tile_receives(way, d))
                def _():
                    received(way, d, k).wait_recv()
            far_chunk(k)
            if k < PARTS - 2:
                near_part(k + 1)
        near_part(PARTS - 1)

        def body(c, carry):
            for r in range(tile_rows):
                level = codes_s[0, s, r, level_at, c]
                at = block_rows(c * tile_rows + r)
                mean = jnp.where(level == 1, near_acc[at, :], far_acc[at, :])
                out[r, c] = (near[2 + r, 2 + c].astype(jnp.float32) - mean).astype(jnp.bfloat16)
            return carry

        lax.fori_loop(0, tile_cols, body, 0)

    @pl.when(is_end)
    def _():
        for part in range(PARTS):
            near_part(part)
        for k in range(chunks):
            white_copy(k).wait_recv()

            def body(c, carry):
                for r in range(tile_rows):
                    level = codes_s[0, s, r, level_at, c]
                    mean = near_acc[block_rows(c * tile_rows + r), :]
                    fine = near[2 + r, 2 + c].astype(jnp.float32) - mean
                    coarse = white_dst[r, c].astype(jnp.float32)
                    out[r, c] = jnp.where(level == 1, fine, coarse).astype(jnp.bfloat16)
                return carry

            lax.fori_loop(starts[k], starts[k + 1], body, 0)

    code_partner.wait_send()

    @pl.when(is_end)
    def _():
        code_straight.wait_send()

    for di, dx in corners:
        @pl.when(present(di, 0) & present(0, dx))
        def _():
            corner_copy(di, dx).wait_send()

    for di, dx in offsets:
        @pl.when(side_sends(di, dx))
        def _():
            side_copy(di, dx).wait_send()
    for which in (0, 1):
        factor_copy(which).wait_send()
    for d in range(n_rows - 2):
        for way in (0, 1):
            @pl.when(tile_sends(way, d))
            def _():
                for k in range(chunks):
                    sent(way, d, k).wait_send()

    @pl.when(is_helper)
    def _():
        code_relay.wait_send()
        for k in range(chunks):
            white_copy(k).wait_send()


def on_device(convergence, block_level, near_codes, far_rows, near_factor, far_factor):
    tile_rows, tile_cols, samples, pixels = convergence.shape
    n_rows, n_cols = lax.axis_size("rows"), lax.axis_size("cols")
    near_slots, far_slots = near_codes.shape[2], far_rows.shape[2]
    half = samples // 2
    starts = chunk_starts(tile_cols)
    chunks = len(starts) - 1
    codes = jnp.concatenate(
        [jnp.transpose(near_codes, (0, 2, 1)), jnp.transpose(far_rows, (0, 2, 1)), block_level[:, None, :]], axis=1)
    codes = jnp.pad(codes, ((0, 0), (0, -codes.shape[1] % 8), (0, -tile_cols % 128)))
    dims = (n_rows, n_cols, tile_rows, tile_cols, half, pixels, near_slots, far_slots)
    block = (half, pixels)
    bf16, f32 = jnp.bfloat16, jnp.float32
    all_rows = tile_rows * tile_cols * half
    chunk_rows = tile_rows * half * max(starts[k + 1] - starts[k] for k in range(chunks))
    dma = pltpu.SemaphoreType.DMA
    scratch = [pltpu.VMEM((n_rows * tile_rows, starts[k + 1] - starts[k]) + block, bf16) for k in range(chunks)]
    scratch += [
        pltpu.VMEM((tile_rows + 4, tile_cols + 4) + block, bf16),
        pltpu.VMEM((2,) + near_factor.shape, bf16),
        pltpu.VMEM((2,) + far_factor.shape, bf16),
        pltpu.VMEM((2, 2) + codes.shape, jnp.int32),
        pltpu.SMEM((2, 2) + codes.shape, jnp.int32),
        pltpu.VMEM((all_rows, 2 * near_slots // PARTS * pixels), bf16),
        pltpu.VMEM((2 * chunk_rows, 2 * far_slots * pixels), bf16),
        pltpu.VMEM((all_rows, pixels), f32),
        pltpu.VMEM((all_rows, pixels), f32),
        pltpu.VMEM((chunk_rows, pixels), f32),
        pltpu.VMEM((tile_rows, tile_cols) + block, bf16),
        pltpu.VMEM((tile_rows, tile_cols) + block, bf16),
        dma((2, n_rows - 2, chunks)),
        dma((2, n_rows - 2, chunks)),
        dma((chunks,)),
        dma((chunks,)),
        dma((4,)),
        dma((4,)),
        dma((4,)),
        dma((4,)),
        dma((3,)),
        dma((3,)),
        dma((2,)),
        dma((2,)),
        dma((6 + chunks,)),
        dma((2, chunks)),
    ]
    anywhere = pl.BlockSpec(memory_space=pl.ANY)
    vmem = pl.BlockSpec(memory_space=pltpu.VMEM)
    return pl.pallas_call(
        functools.partial(kernel, dims),
        out_shape=jax.ShapeDtypeStruct((tile_rows, tile_cols) + block, bf16),
        in_specs=[anywhere, vmem, anywhere, anywhere],
        out_specs=vmem,
        scratch_shapes=scratch,
        compiler_params=pltpu.CompilerParams(
            collective_id=0, has_side_effects=True, vmem_limit_bytes=56 * 1024 * 1024),
    )(convergence, codes, near_factor, far_factor)


def solution(mesh):
    placed = (
        P(("fields", "rows"), "cols", None, None),
        P(("fields", "rows"), "cols"),
        P(("fields", "rows"), "cols", "sub"),
        P(("fields", "rows"), "cols", "sub"),
        P(None, "sub"),
        P(None, "sub"),
    )
    return jax.shard_map(
        on_device,
        mesh=mesh,
        in_specs=placed,
        out_specs=P(("fields", "rows"), "cols", "sub", None),
        check_vma=False,
    )
```

```python
import functools

import jax
import jax.numpy as jnp
from jax import lax
from jax.experimental import pallas as pl
from jax.experimental.pallas import tpu as pltpu
from jax.sharding import PartitionSpec as P

MESH = pl.DeviceIdType.MESH
PARTS = 4


def chunk_starts(cols):
    return [0, cols * 5 // 16, cols * 10 // 16, cols * 14 // 16, cols]


def kernel(dims, conv, codes, near_factor, far_factor, out, *scratch):
    n_rows, n_cols, tile_rows, tile_cols, half, pixels, near_slots, far_slots = dims
    starts = chunk_starts(tile_cols)
    chunks = len(starts) - 1
    sizes = [starts[k + 1] - starts[k] for k in range(chunks)]
    far = scratch[:chunks]
    (near, near_w, far_w, codes_v, codes_s, near_g, far_g, near_acc, far_acc, end_acc,
     white_src, white_dst, tile_send, tile_recv, white_send, white_recv,
     side_send, side_recv, corner_send, corner_recv, code_send, code_recv, fac_send, fac_recv, loc_sem, halo_sem) = scratch[chunks:]

    i = lax.axis_index("rows")
    x = lax.axis_index("cols")
    s = lax.axis_index("sub")
    other = 1 - s
    mine = pl.ds(pl.multiple_of(s * half, half), half)
    is_end = (i == 0) | (i == n_rows - 1)
    is_mid = (i > 0) & (i < n_rows - 1)
    low_helper = i == 1
    high_helper = i == n_rows - 2
    is_helper = low_helper | high_helper
    end_tile = jnp.where(low_helper, 0, n_rows - 1)
    to_mid = jnp.where(i == 0, 1, n_rows - 2)

    def cols_of(k):
        return pl.ds(starts[k], sizes[k])

    local = [
        pltpu.make_async_copy(
            conv.at[:, :, mine, :],
            near.at[pl.ds(2, tile_rows), pl.ds(2, tile_cols)],
            loc_sem.at[0],
        ),
        pltpu.make_async_copy(near_factor, near_w.at[s], loc_sem.at[1]),
        pltpu.make_async_copy(far_factor, far_w.at[s], loc_sem.at[2]),
        pltpu.make_async_copy(codes, codes_s.at[0, s], loc_sem.at[3]),
    ]
    for copy in local:
        copy.start()
    own_far = [
        pltpu.make_async_copy(
            conv.at[:, cols_of(k), mine, :],
            far[k].at[pl.ds(i * tile_rows, tile_rows)],
            loc_sem.at[6 + k],
        )
        for k in range(chunks)
    ]

    @pl.when(is_mid)
    def _():
        for copy in own_far:
            copy.start()

    @pl.when(i == 0)
    def _():
        near[0:2] = jnp.zeros((2,) + near.shape[1:], near.dtype)

    @pl.when(i == n_rows - 1)
    def _():
        near[tile_rows + 2:tile_rows + 4] = jnp.zeros((2,) + near.shape[1:], near.dtype)

    @pl.when(x == 0)
    def _():
        near[:, 0:2] = jnp.zeros((near.shape[0], 2) + near.shape[2:], near.dtype)

    @pl.when(x == n_cols - 1)
    def _():
        near[:, tile_cols + 2:tile_cols + 4] = jnp.zeros((near.shape[0], 2) + near.shape[2:], near.dtype)

    barrier = pltpu.get_barrier_semaphore()
    offsets = [(-1, 0), (1, 0), (0, -1), (0, 1)]

    def present(di, dx):
        ok = jnp.bool_(True)
        if di == -1:
            ok = ok & (i > 0)
        if di == 1:
            ok = ok & (i < n_rows - 1)
        if dx == -1:
            ok = ok & (x > 0)
        if dx == 1:
            ok = ok & (x < n_cols - 1)
        return ok

    for di, dx in offsets:
        @pl.when(present(di, dx))
        def _():
            pl.semaphore_signal(barrier, inc=1, device_id={"rows": i + di, "cols": x + dx}, device_id_type=MESH)
    pl.semaphore_signal(barrier, inc=1, device_id={"sub": other}, device_id_type=MESH)
    count_z = (i > 0).astype(jnp.int32) + (i < n_rows - 1).astype(jnp.int32)
    count_x = (x > 0).astype(jnp.int32) + (x < n_cols - 1).astype(jnp.int32)
    pl.semaphore_wait(barrier, count_z + count_x + 1)

    def code_copy(which, slot, target):
        return pltpu.make_async_remote_copy(
            src_ref=codes if which < 2 else codes_v.at[slot, s], dst_ref=codes_v.at[slot, s],
            send_sem=code_send.at[which], recv_sem=code_recv.at[which], device_id=target, device_id_type=MESH)

    code_partner = code_copy(0, 0, {"sub": other})
    code_straight = code_copy(1, 1, {"rows": to_mid})
    code_relay = code_copy(2, 1, {"sub": other})
    code_partner.start()

    @pl.when(is_end)
    def _():
        code_straight.start()

    def side_copy(di, dx):
        if di == 0:
            rows_src, rows_dst = pl.ds(0, tile_rows), pl.ds(2, tile_rows)
        elif di == -1:
            rows_src, rows_dst = pl.ds(0, 2), pl.ds(tile_rows + 2, 2)
        else:
            rows_src, rows_dst = pl.ds(tile_rows - 2, 2), pl.ds(0, 2)
        if dx == 0:
            cols_src, cols_dst = pl.ds(0, tile_cols), pl.ds(2, tile_cols)
        elif dx == -1:
            cols_src, cols_dst = pl.ds(0, 2), pl.ds(tile_cols + 2, 2)
        else:
            cols_src, cols_dst = pl.ds(tile_cols - 2, 2), pl.ds(0, 2)
        which = offsets.index((di, dx))
        return pltpu.make_async_remote_copy(
            src_ref=conv.at[rows_src, cols_src, mine, :],
            dst_ref=near.at[rows_dst, cols_dst],
            send_sem=side_send.at[which], recv_sem=side_recv.at[which],
            device_id={"rows": i + di, "cols": x + dx}, device_id_type=MESH)

    def side_sends(di, dx):
        if dx == 0:
            return low_helper if di == -1 else high_helper
        return present(di, dx)

    def side_receives(di, dx):
        if dx == 0:
            return (i == 0) if di == -1 else (i == n_rows - 1)
        return present(-di, -dx)

    def tile_copy(way, d, k, tile):
        src = conv.at[:, cols_of(k), mine, :] if d == 0 else far[k].at[pl.ds(tile * tile_rows, tile_rows)]
        return pltpu.make_async_remote_copy(
            src_ref=src, dst_ref=far[k].at[pl.ds(tile * tile_rows, tile_rows)],
            send_sem=tile_send.at[way, d, k], recv_sem=tile_recv.at[way, d, k],
            device_id={"rows": i - 1 if way == 0 else i + 1}, device_id_type=MESH)

    def sent(way, d, k):
        return tile_copy(way, d, k, i + d if way == 0 else i - d)

    def received(way, d, k):
        return tile_copy(way, d, k, i + 1 + d if way == 0 else i - 1 - d)

    def tile_sends(way, d):
        if way == 0:
            return (i >= 2) & (i + d <= n_rows - 1)
        return (i <= n_rows - 3) & (i - d >= 0)

    def tile_receives(way, d):
        if way == 0:
            return is_mid & (i + 1 + d <= n_rows - 1)
        return is_mid & (i - 1 - d >= 0)

    for k in range(chunks):
        for way in (0, 1):
            @pl.when(tile_sends(way, 0))
            def _():
                sent(way, 0, k).start()
        if k == 0:
            for di, dx in offsets:
                @pl.when(side_sends(di, dx))
                def _():
                    side_copy(di, dx).start()

    def factor_copy(which):
        src, dst = ((near_factor, near_w), (far_factor, far_w))[which]
        return pltpu.make_async_remote_copy(
            src_ref=src, dst_ref=dst.at[s], send_sem=fac_send.at[which],
            recv_sem=fac_recv.at[which], device_id={"sub": other}, device_id_type=MESH)

    for which in (0, 1):
        factor_copy(which).start()

    def halo_copy(way, k):
        if way == 0:
            src_rows, dst_rows = pl.ds((i + 1) * tile_rows, 2), pl.ds(tile_rows + 2, 2)
        else:
            src_rows, dst_rows = pl.ds(i * tile_rows - 2, 2), pl.ds(0, 2)
        return pltpu.make_async_copy(
            far[k].at[src_rows], near.at[dst_rows, pl.ds(2 + starts[k], sizes[k])], halo_sem.at[way, k])

    for d in range(n_rows - 3):
        for k in range(chunks):
            for way in (0, 1):
                @pl.when(tile_receives(way, d))
                def _():
                    received(way, d, k).wait_recv()
                    if d == 0:
                        halo_copy(way, k).start()

                @pl.when(tile_sends(way, d + 1))
                def _():
                    sent(way, d + 1, k).start()

    code_copy(0, 0, {"sub": other}).wait_recv()
    code_in = pltpu.make_async_copy(codes_v.at[0, other], codes_s.at[0, other], loc_sem.at[4])
    code_in.start()
    end_codes = pltpu.make_async_copy(codes_v.at[1], codes_s.at[1], loc_sem.at[5])

    @pl.when(is_helper)
    def _():
        code_straight.wait_recv()
        code_relay.start()

    for copy in local:
        copy.wait()

    @pl.when(is_mid)
    def _():
        for k in range(chunks):
            halo_copy(0, k).wait()
            halo_copy(1, k).wait()
            own_far[k].wait()

    for di, dx in offsets:
        @pl.when(side_receives(di, dx))
        def _():
            side_copy(di, dx).wait_recv()

    def corner_copy(di, dx):
        rows = pl.ds(0, 2) if di == -1 else pl.ds(tile_rows + 2, 2)
        src, dst = (2, tile_cols + 2) if dx == -1 else (tile_cols, 0)
        which = (di + 1) + (dx + 1) // 2
        return pltpu.make_async_remote_copy(
            src_ref=near.at[rows, pl.ds(src, 2)], dst_ref=near.at[rows, pl.ds(dst, 2)],
            send_sem=corner_send.at[which], recv_sem=corner_recv.at[which],
            device_id={"cols": x + dx}, device_id_type=MESH)

    corners = [(di, dx) for di in (-1, 1) for dx in (-1, 1)]
    for di, dx in corners:
        @pl.when(present(di, 0) & present(0, dx))
        def _():
            corner_copy(di, dx).start()

    @pl.when(is_helper)
    def _():
        code_relay.wait_recv()
        end_codes.start()
        end_codes.wait()

    code_in.wait()
    for which in (0, 1):
        factor_copy(which).wait_recv()
    for di, dx in corners:
        @pl.when(present(di, 0) & present(0, -dx))
        def _():
            corner_copy(di, dx).wait_recv()

    contract = (((1,), (1,)), ((), ()))
    part_slots = 2 * near_slots // PARTS

    def block_rows(block):
        return pl.ds(pl.multiple_of(block * half, half), half)

    def pair_rows(block):
        return pl.ds(pl.multiple_of(block * half, 2 * half), 2 * half)

    def joined(first, second):
        both = jnp.concatenate([first.astype(jnp.float32), second.astype(jnp.float32)], axis=0)
        return both.astype(jnp.bfloat16)

    def near_part(part):
        sub, base = part * part_slots // near_slots, part * part_slots % near_slots

        def near_block(r, c, slot):
            code = codes_s[0, sub, r, base + slot, c]
            down = lax.shift_right_logical(code * 205, 10)
            return near[r + down, c + code - 5 * down]

        def gather(c, carry):
            for r in range(0, tile_rows, 2):
                for slot in range(part_slots):
                    near_g[pair_rows(c * tile_rows + r), slot * pixels:(slot + 1) * pixels] = joined(
                        near_block(r, c, slot), near_block(r + 1, c, slot))
            return carry

        lax.fori_loop(0, tile_cols, gather, 0)
        product = lax.dot_general(
            near_g[...], near_w[sub, :, base * pixels:(base + part_slots) * pixels], contract,
            preferred_element_type=jnp.float32)
        if part == 0:
            near_acc[...] = product
        else:
            near_acc[...] += product

    level_at = near_slots + far_slots

    def far_chunk(k):
        rows = sizes[k] * tile_rows * half

        def gather_far(who):
            def far_block(r, c, sub, slot):
                row = codes_s[who, sub, r, near_slots + slot, starts[k] + c]
                return far[k][row, c]

            def body(c, carry):
                for r in range(0, tile_rows, 2):
                    for sub in range(2):
                        for slot in range(far_slots):
                            at = sub * far_slots + slot
                            far_g[pair_rows((who * sizes[k] + c) * tile_rows + r), at * pixels:(at + 1) * pixels] = joined(
                                far_block(r, c, sub, slot), far_block(r + 1, c, sub, slot))
                return carry

            lax.fori_loop(0, sizes[k], body, 0)

        gather_far(0)

        @pl.when(is_helper)
        def _():
            gather_far(1)

        depth = far_slots * pixels
        product = lax.dot_general(
            far_g[:2 * rows, :depth], far_w[0], contract, preferred_element_type=jnp.float32)
        product += lax.dot_general(
            far_g[:2 * rows, depth:], far_w[1], contract, preferred_element_type=jnp.float32)
        far_acc[pl.ds(starts[k] * tile_rows * half, rows), :] = product[:rows]
        end_acc[pl.ds(0, rows), :] = product[rows:]

        @pl.when(is_helper)
        def _():
            def body(c, carry):
                for r in range(tile_rows):
                    value = far[k][end_tile * tile_rows + r, c].astype(jnp.float32)
                    white_src[r, starts[k] + c] = (value - end_acc[block_rows(c * tile_rows + r), :]).astype(jnp.bfloat16)
                return carry

            lax.fori_loop(0, sizes[k], body, 0)
            white_copy(k).start()

    def white_copy(k):
        return pltpu.make_async_remote_copy(
            src_ref=white_src.at[:, cols_of(k)], dst_ref=white_dst.at[:, cols_of(k)],
            send_sem=white_send.at[k], recv_sem=white_recv.at[k],
            device_id={"rows": end_tile}, device_id_type=MESH)

    @pl.when(is_mid)
    def _():
        near_part(0)
        for k in range(chunks):
            d = n_rows - 3
            for way in (0, 1):
                @pl.when(tile_receives(way, d))
                def _():
                    received(way, d, k).wait_recv()
            far_chunk(k)
            if k < PARTS - 2:
                near_part(k + 1)
        near_part(PARTS - 1)

        def body(c, carry):
            for r in range(tile_rows):
                level = codes_s[0, s, r, level_at, c]
                at = block_rows(c * tile_rows + r)
                mean = jnp.where(level == 1, near_acc[at, :], far_acc[at, :])
                out[r, c] = (near[2 + r, 2 + c].astype(jnp.float32) - mean).astype(jnp.bfloat16)
            return carry

        lax.fori_loop(0, tile_cols, body, 0)

    @pl.when(is_end)
    def _():
        for part in range(PARTS):
            near_part(part)
        for k in range(chunks):
            white_copy(k).wait_recv()

            def body(c, carry):
                for r in range(tile_rows):
                    level = codes_s[0, s, r, level_at, c]
                    mean = near_acc[block_rows(c * tile_rows + r), :]
                    fine = near[2 + r, 2 + c].astype(jnp.float32) - mean
                    coarse = white_dst[r, c].astype(jnp.float32)
                    out[r, c] = jnp.where(level == 1, fine, coarse).astype(jnp.bfloat16)
                return carry

            lax.fori_loop(starts[k], starts[k + 1], body, 0)

    code_partner.wait_send()

    @pl.when(is_end)
    def _():
        code_straight.wait_send()

    for di, dx in corners:
        @pl.when(present(di, 0) & present(0, dx))
        def _():
            corner_copy(di, dx).wait_send()

    for di, dx in offsets:
        @pl.when(side_sends(di, dx))
        def _():
            side_copy(di, dx).wait_send()
    for which in (0, 1):
        factor_copy(which).wait_send()
    for d in range(n_rows - 2):
        for way in (0, 1):
            @pl.when(tile_sends(way, d))
            def _():
                for k in range(chunks):
                    sent(way, d, k).wait_send()

    @pl.when(is_helper)
    def _():
        code_relay.wait_send()
        for k in range(chunks):
            white_copy(k).wait_send()


def on_device(convergence, block_level, near_codes, far_rows, near_factor, far_factor):
    tile_rows, tile_cols, samples, pixels = convergence.shape
    n_rows, n_cols = lax.axis_size("rows"), lax.axis_size("cols")
    near_slots, far_slots = near_codes.shape[2], far_rows.shape[2]
    half = samples // 2
    starts = chunk_starts(tile_cols)
    chunks = len(starts) - 1
    codes = jnp.concatenate(
        [jnp.transpose(near_codes, (0, 2, 1)), jnp.transpose(far_rows, (0, 2, 1)), block_level[:, None, :]], axis=1)
    dims = (n_rows, n_cols, tile_rows, tile_cols, half, pixels, near_slots, far_slots)
    block = (half, pixels)
    bf16, f32 = jnp.bfloat16, jnp.float32
    all_rows = tile_rows * tile_cols * half
    chunk_rows = tile_rows * half * max(starts[k + 1] - starts[k] for k in range(chunks))
    dma = pltpu.SemaphoreType.DMA
    scratch = [pltpu.VMEM((n_rows * tile_rows, starts[k + 1] - starts[k]) + block, bf16) for k in range(chunks)]
    scratch += [
        pltpu.VMEM((tile_rows + 4, tile_cols + 4) + block, bf16),
        pltpu.VMEM((2,) + near_factor.shape, bf16),
        pltpu.VMEM((2,) + far_factor.shape, bf16),
        pltpu.VMEM((2, 2) + codes.shape, jnp.int32),
        pltpu.SMEM((2, 2) + codes.shape, jnp.int32),
        pltpu.VMEM((all_rows, 2 * near_slots // PARTS * pixels), bf16),
        pltpu.VMEM((2 * chunk_rows, 2 * far_slots * pixels), bf16),
        pltpu.VMEM((all_rows, pixels), f32),
        pltpu.VMEM((all_rows, pixels), f32),
        pltpu.VMEM((chunk_rows, pixels), f32),
        pltpu.VMEM((tile_rows, tile_cols) + block, bf16),
        pltpu.VMEM((tile_rows, tile_cols) + block, bf16),
        dma((2, n_rows - 2, chunks)),
        dma((2, n_rows - 2, chunks)),
        dma((chunks,)),
        dma((chunks,)),
        dma((4,)),
        dma((4,)),
        dma((4,)),
        dma((4,)),
        dma((3,)),
        dma((3,)),
        dma((2,)),
        dma((2,)),
        dma((6 + chunks,)),
        dma((2, chunks)),
    ]
    anywhere = pl.BlockSpec(memory_space=pl.ANY)
    vmem = pl.BlockSpec(memory_space=pltpu.VMEM)
    return pl.pallas_call(
        functools.partial(kernel, dims),
        out_shape=jax.ShapeDtypeStruct((tile_rows, tile_cols) + block, bf16),
        in_specs=[anywhere, vmem, anywhere, anywhere],
        out_specs=vmem,
        scratch_shapes=scratch,
        compiler_params=pltpu.CompilerParams(
            collective_id=0, has_side_effects=True, vmem_limit_bytes=56 * 1024 * 1024),
    )(convergence, codes, near_factor, far_factor)


def solution(mesh):
    placed = (
        P(("fields", "rows"), "cols", None, None),
        P(("fields", "rows"), "cols"),
        P(("fields", "rows"), "cols", "sub"),
        P(("fields", "rows"), "cols", "sub"),
        P(None, "sub"),
        P(None, "sub"),
    )
    return jax.shard_map(
        on_device,
        mesh=mesh,
        in_specs=placed,
        out_specs=P(("fields", "rows"), "cols", "sub", None),
        check_vma=False,
    )
```
